512 devices in a mesh: frames: 32 (over x, y_lo, core), book: 16 (over z, y_hi).
Axes of the slice: x: 4, y: 8 (y_hi: 2, y_lo: 4; y = y_hi * 4 + y_lo), z: 8, core: 2. Of those that a mesh axis runs over, the one named last changes fastest.
Arguments:
- gate_pre: bfloat16 [8192, 6144], P('frames', 'book'), may hold values from -6 to 6
- up_pre: bfloat16 [8192, 6144], P('frames', 'book'), may hold values from -6 to 6
- down_weight: bfloat16 [6144, 4096], P('book'), may hold values from -0.109375 to 0.109375
- residual: bfloat16 [8192, 4096], P('frames', 'book'), may hold values from -6 to 6
- out_gain: bfloat16 [4096], replicated, may hold values from 0.25 to 1.75
- in_proj: bfloat16 [16, 4096, 1024], P('book', 'frames'), may hold values from -0.09375 to 0.09375
- embedding: bfloat16 [16, 1024, 1024], P('book', 'frames'), may hold values from -6 to 6
- token_ids: int32 [8192, 16], P('frames', 'book'), may hold values from 0 to 1023
- depth_gain: bfloat16 [16, 1024], P('book'), may hold values from 0.25 to 1.75
- qkv_weight: bfloat16 [16, 1024, 1536], P('book', 'frames'), may hold values from -2 to 2
Outputs:
- context: bfloat16 [8192, 16, 512], P(('frames', 'book'))
The draws below stay inside these ranges and needn't reach their ends.
All inputs are finite; a program needn't handle non-finite values.
Results may differ from the reference program's by a relative error of at most 0.019.
Values may be sent and summed in bfloat16 or wider, within the bound.
A program may use at most 64 MiB of HBM per device.

```python
import math
import jax
import jax.numpy as jnp
from jax import lax

D = 4096
FFW = 6144
DD = 1024
H = 8
HD = 64
V = 1024
FR_DEV = 256
K = 16
FRAMES = 8192
N_FRAMES = 32


def draw_qkv_weight(key, part):
    first_key = jax.random.fold_in(jax.random.fold_in(key, 11), 0)
    width = H * HD
    drawn = jax.random.normal(first_key, (K, DD, 3 * width), jnp.float32) / math.sqrt(DD)
    return jnp.clip(drawn, -2.0, 2.0).astype(jnp.bfloat16)


def with_ends(array, rng, low, high):
    shape = array.shape
    index_at = [jax.random.randint(jax.random.fold_in(rng, axis), (), 0, shape[axis]) for axis in range(len(shape))]
    array = array.at[tuple(index_at)].set(low)
    longest = shape.index(max(shape))
    index_at[longest] = (index_at[longest] + 1) % shape[longest]
    return array.at[tuple(index_at)].set(high)


def with_spikes(result, key, source, target, blocks, factor):
    owner, partner = [(jnp.arange(result.shape[axis_at]) // (result.shape[axis_at] // blocks)).reshape([-1 if axis == axis_at else 1 for axis in range(result.ndim)]) for axis_at in (source, target)]
    chosen = jax.random.permutation(key, blocks)[partner]
    strong = (owner == chosen) | (owner == (partner + blocks // 2) % blocks)
    return jnp.where(strong, factor * result, result)


def level_of(rng, dims, cuts, least, high):
    def one(axis_at, blocks):
        steps = jax.random.uniform(jax.random.fold_in(jax.random.fold_in(rng, 6), axis_at), (blocks,), jnp.float32, least / len(cuts), high / len(cuts))
        return jnp.repeat(jnp.exp(steps), dims[axis_at] // blocks).reshape((-1,) + (1,) * (len(dims) - axis_at - 1))

    loudness = one(*cuts[0])
    for cut in cuts[1:]:
        loudness = loudness * one(*cut)
    return loudness


def centred(own_key, shape, deviation, reach, cuts=(), held_as=jnp.bfloat16):
    level = level_of(own_key, shape, cuts, -0.22, 0.18) if cuts else 1.0
    entries = jax.random.normal(own_key, shape, jnp.float32) * deviation * level
    return jnp.minimum(jnp.maximum(entries, -reach), reach).astype(held_as)


def bell_draw_with(rng, dims, scale, reach, cuts, heavy, held_as=jnp.bfloat16):
    values = scale * jax.random.normal(rng, dims, jnp.float32)
    if cuts:
        values = values * level_of(rng, dims, cuts, -0.22, 0.18)
    return jnp.clip(with_spikes(values, jax.random.fold_in(rng, 3), *heavy), -reach, reach).astype(held_as)


def setup_inputs(seed: int = 0) -> dict:
    splits = jax.random.split(jax.random.key(seed), 11)
    gate_pre = centred(splits[0], (FRAMES, FFW), 1.0, 6.0, ((0, 32), (1, 16)))
    up_pre = centred(splits[1], (FRAMES, FFW), 1.0, 6.0, ((0, 32), (1, 16)))
    down_weight = bell_draw_with(splits[2], (FFW, D), FFW ** -0.5, 0.109375, ((0, 16),), (0, 1, 16, 2.0))
    residual = centred(splits[3], (FRAMES, D), 1.0, 6.0, ((0, 32), (1, 16)))
    out_gain = jnp.clip(1.0 + 0.15 * jax.random.normal(splits[4], (D,), jnp.float32), 0.25, 1.75).astype(jnp.bfloat16)
    in_proj = centred(splits[5], (K, D, DD), D ** -0.5, 0.09375, ((0, 16), (1, 32)))
    embedding = centred(splits[6], (K, V, DD), 1.0, 6.0, ((0, 16), (1, 32)))
    token_ids = with_ends(jax.random.randint(splits[7], (FRAMES, K), 0, V), jax.random.fold_in(splits[7], 1), 0, V - 1).astype(jnp.int32)
    depth_gain = jnp.clip(1.0 + 0.15 * jax.random.normal(splits[8], (K, DD), jnp.float32), 0.25, 1.75).astype(jnp.bfloat16)
    qkv_weight = draw_qkv_weight(jax.random.fold_in(splits[10], 71), 0)
    return {"gate_pre": gate_pre, "up_pre": up_pre, "down_weight": down_weight, "residual": residual, "out_gain": out_gain, "in_proj": in_proj, "embedding": embedding, "token_ids": token_ids, "depth_gain": depth_gain, "qkv_weight": qkv_weight}


def rms_scale(values, gain):
    moment = lax.optimization_barrier(jnp.mean(values * values, axis=-1, keepdims=True))
    return values * lax.rsqrt(moment + 1e-05) * gain

def attend_frames(packed):
    frames_here = packed.shape[0]
    width = H * HD
    queries = packed[:, :, :width].reshape(frames_here, K, H, HD).astype(jnp.float32)
    keys_all = packed[:, :, width:2 * width].reshape(frames_here, K, H, HD).astype(jnp.float32)
    values_all = packed[:, :, 2 * width:].reshape(frames_here, K, H, HD).astype(jnp.float32)
    scores = jnp.einsum('nkhd,njhd->nhkj', queries, keys_all) * HD ** (-0.5)
    causal = jnp.arange(K)[:, None] >= jnp.arange(K)[None, :]
    scores = jnp.where(causal, scores, -1e+30)
    peak = lax.optimization_barrier(jnp.max(scores, axis=-1, keepdims=True))
    expo = jnp.exp(scores - peak)
    probability = lax.optimization_barrier((expo / lax.optimization_barrier(jnp.sum(expo, axis=-1, keepdims=True))).astype(jnp.bfloat16))
    context = jnp.einsum('nhkj,njhd->nkhd', probability.astype(jnp.float32), values_all)
    return context.reshape(frames_here, K, width).astype(jnp.bfloat16)

def reference(gate_pre, up_pre, down_weight, residual, out_gain, in_proj, embedding, token_ids, depth_gain, qkv_weight):
    hidden = (jax.nn.silu(gate_pre.astype(jnp.float32)) * up_pre.astype(jnp.float32)).astype(jnp.bfloat16)
    temporal = (jnp.dot(hidden, down_weight, preferred_element_type=jnp.float32) + residual.astype(jnp.float32)).astype(jnp.bfloat16)
    normed = rms_scale(temporal.astype(jnp.float32), out_gain.astype(jnp.float32)).astype(jnp.bfloat16)

    def per_book(book_index):
        projected = jnp.dot(normed, in_proj[book_index], preferred_element_type=jnp.float32)
        looked = jnp.take(embedding[book_index], token_ids[:, book_index], axis=0).astype(jnp.float32)
        depth_in = (projected + looked).astype(jnp.bfloat16)
        depth_normed = rms_scale(depth_in.astype(jnp.float32), depth_gain[book_index].astype(jnp.float32)).astype(jnp.bfloat16)
        return jnp.dot(depth_normed, qkv_weight[book_index], preferred_element_type=jnp.float32).astype(jnp.bfloat16)
    packed = lax.map(per_book, jnp.arange(K, dtype=jnp.int32))
    packed = jnp.transpose(packed, (1, 0, 2))
    blocks = packed.reshape(N_FRAMES, FR_DEV, K, packed.shape[2])
    context = lax.map(attend_frames, blocks)
    return context.reshape(FRAMES, K, H * HD)
```

```python
import functools

import jax
import jax.numpy as jnp
from jax import lax
from jax.experimental import pallas as pl
from jax.experimental.pallas import tpu as pltpu
from jax.sharding import PartitionSpec as P

H = 8
HD = 64
WIDTH = H * HD
MESH = pl.DeviceIdType.MESH
F32 = jnp.float32
BF16 = jnp.bfloat16


def coords():
    f = lax.axis_index("frames")
    b = lax.axis_index("book")
    core = lax.rem(f, 2)
    y_lo = lax.rem(f // 2, 4)
    x = f // 8
    return x, lax.rem(b, 2) * 4 + y_lo, b // 2, core


def dev(x, y, z, core):
    return {"frames": x * 8 + lax.rem(y, 4) * 2 + core, "book": z * 2 + y // 4}


def send(src, dst, ssem, rsem, target):
    return pltpu.make_async_remote_copy(
        src_ref=src, dst_ref=dst, send_sem=ssem, recv_sem=rsem,
        device_id=target, device_id_type=MESH,
    )


def mod8(v):
    return lax.rem(v + 16, 8)


def barrier(targets, count):
    sem = pltpu.get_barrier_semaphore()
    for target in targets:
        pl.semaphore_signal(sem, inc=1, device_id=target, device_id_type=MESH)
    pl.semaphore_wait(sem, count)


def mix_kernel(gate, up, dw, res, out, hid, own, a_s, a_r, zs, ys, y_rel, y_r, tf,
               a_ss, a_rs, y_ss, y_rs, b_ss, b_rs, o_sem):
    x, y, z, core = coords()
    y_hi = y // 4
    zn = (dev(x, y, mod8(z + 1), core), dev(x, y, mod8(z - 1), core))
    yn = (dev(x, mod8(y + 2), z, core), dev(x, mod8(y - 2), z, core))
    barrier(zn + yn, 4)

    g = gate[...].astype(F32)
    hid[...] = (g / (1.0 + jnp.exp(-g)) * up[...].astype(F32)).astype(BF16)
    sent = []

    def a_copy(d, u, s):
        return send(a_s.at[d, u, s], a_r.at[d, u, s], a_ss.at[d, u, s], a_rs.at[d, u, s], zn[d])

    def y_copy(d, u):
        return send(ys.at[d, u], y_rel.at[d, u], y_ss.at[0, d, u], y_rs.at[0, d, u], yn[d])

    def y_copy2(d, u):
        return send(y_rel.at[d, u], y_r.at[d, u], y_ss.at[1, d, u], y_rs.at[1, d, u], yn[d])

    for s in range(8):
        for d in (0, 1):
            blk = mod8(z - 1 - s) if d == 0 else mod8(z + 1 + s)
            cols = pl.ds(pl.multiple_of(blk * 512, 512), 512)
            own[d] = jnp.dot(hid[d * 128:(d + 1) * 128, :], dw[:, cols],
                             preferred_element_type=F32).reshape(2, 64, 512)
        for u in (0, 1):
            for d in (0, 1):
                val = own[d, u]
                if s > 0:
                    a_copy(d, u, s - 1).wait_recv()
                    val = val + a_r[d, u, s - 1].astype(F32)
                if s < 7:
                    a_s[d, u, s] = val.astype(BF16)
                    copy = a_copy(d, u, s)
                    copy.start()
                    sent.append(copy)
                else:
                    zs[d, u] = val
                    cols = pl.ds(pl.multiple_of(y_hi * 256, 256), 256)
                    rows = pl.ds(d * 128 + u * 64, 64)
                    zs[d, u, :, cols] = zs[d, u, :, cols] + res[rows, :].astype(F32)
                    ys[d, u] = zs[d, u].astype(BF16)
                    copy = y_copy(d, u)
                    copy.start()
                    sent.append(copy)
    for u in (0, 1):
        for d in (0, 1):
            y_copy(d, u).wait_recv()
            copy = y_copy2(d, u)
            copy.start()
            sent.append(copy)

    def b_copy(d, s, h):
        blk = mod8(z - s) if d == 0 else mod8(z + s)
        ref = tf.at[blk, h]
        return send(ref, ref, b_ss.at[d, s, h], b_rs.at[d, s, h], zn[d])

    for d in (0, 1):
        for u in (0, 1):
            y_copy2(d, u).wait_recv()
            tf[z, d, u * 64:(u + 1) * 64, :] = (zs[d, u] + y_r[d, u].astype(F32)).astype(BF16)
        for way in (0, 1):
            copy = b_copy(way, 0, d)
            copy.start()
            sent.append(copy)
    for s in range(1, 5):
        for h in (0, 1):
            for d in (0, 1):
                if s == 4 and h != d:
                    continue
                b_copy(d, s - 1, h).wait_recv()
                if s < 3 or (s == 3 and h == d):
                    copy = b_copy(d, s, h)
                    copy.start()
                    sent.append(copy)
    for copy in sent:
        copy.wait_send()
    done = pltpu.make_async_copy(tf, out, o_sem)
    done.start()
    done.wait()


def mix(gate, up, dw, res):
    vmem = pl.BlockSpec(memory_space=pltpu.VMEM)
    dma = pltpu.SemaphoreType.DMA
    return pl.pallas_call(
        mix_kernel,
        name="mix",
        out_shape=jax.ShapeDtypeStruct((8, 2, 128, 512), BF16),
        in_specs=[vmem] * 4,
        out_specs=pl.BlockSpec(memory_space=pl.ANY),
        scratch_shapes=[
            pltpu.VMEM((256, 384), BF16),
            pltpu.VMEM((2, 2, 64, 512), F32),
            pltpu.VMEM((2, 2, 7, 64, 512), BF16),
            pltpu.VMEM((2, 2, 7, 64, 512), BF16),
            pltpu.VMEM((2, 2, 64, 512), F32),
            pltpu.VMEM((2, 2, 64, 512), BF16),
            pltpu.VMEM((2, 2, 64, 512), BF16),
            pltpu.VMEM((2, 2, 64, 512), BF16),
            pltpu.VMEM((8, 2, 128, 512), BF16),
            dma((2, 2, 7)), dma((2, 2, 7)),
            dma((2, 2, 2)), dma((2, 2, 2)),
            dma((2, 4, 2)), dma((2, 4, 2)),
            dma,
        ],
        compiler_params=pltpu.CompilerParams(collective_id=0, has_side_effects=True),
        cost_estimate=pl.CostEstimate(flops=10**9, bytes_accessed=100 * 2**20, transcendentals=0),
    )(gate, up, dw, res)


def depth_kernel(tf, gain, w, emb, tok, dgain, qw, out, xb, acc, packed, q_all, qp, rel,
                 d_ss, d_rs, r_ss, r_rs):
    x, y, z, core = coords()
    y_hi = y // 4
    b = z * 2 + y_hi
    up, down = mod8(y + 2), mod8(y - 2)
    peers = [dev(x, y, mod8(z - i), core) for i in range(1, 8)]
    peers += [dev(x, down, mod8(z - i), core) for i in range(4)]
    peers += [dev(x, up, z, core)]
    peers += [dev(x, up, mod8(z - i), core) for i in range(4, 8)]
    barrier(peers, len(peers))

    acc[...] = jnp.zeros_like(acc)

    def block(i, total):
        v = tf[i].reshape(256, 512).astype(F32)
        xb[...] = (v * gain[i].astype(F32)).astype(BF16)

        def tile(n, carry):
            cols = pl.ds(pl.multiple_of(n * 256, 256), 256)
            rows = pl.ds(pl.multiple_of(i * 512, 512), 512)
            acc[:, cols] += jnp.dot(xb[...], w[rows, cols], preferred_element_type=F32)
            return carry

        lax.fori_loop(0, 4, tile, 0)
        return total + jnp.sum(v * v, axis=-1, keepdims=True)

    total = lax.fori_loop(0, 8, block, jnp.zeros((256, 1), F32))
    scale = lax.rsqrt(total * (1.0 / 4096) + 1e-05)
    columns = lax.broadcasted_iota(jnp.int32, (256, 1024), 1)
    matches = jnp.where(tok[...] == columns, 1.0, 0.0).astype(BF16)
    depth = (acc[...] * scale + jnp.dot(matches, emb[...], preferred_element_type=F32)).astype(BF16)
    depth = depth.astype(F32)
    moment = jnp.mean(depth * depth, axis=-1, keepdims=True)
    normed = (depth * lax.rsqrt(moment + 1e-05) * dgain[...].astype(F32)).astype(BF16)
    packed[...] = jnp.dot(normed, qw[...], preferred_element_type=F32).astype(BF16)

    def rows_of(zz, plane):
        return pl.ds(pl.multiple_of((zz * 2 + plane) * 16, 16), 16)

    def slot(zz, plane):
        return q_all.at[rows_of(zz, plane)]

    sent = []

    def go(copy):
        copy.start()
        sent.append(copy)

    def first(i):
        way = i // 4
        return send(packed.at[rows_of(mod8(z + i), 1 - y_hi)], rel.at[i],
                    r_ss.at[i], r_rs.at[i], dev(x, (up, down)[way], z, core))

    def second(i):
        way = i // 4
        source = (down, up)[way] // 4
        return send(rel.at[i], slot(z, source), d_ss.at[8 + i], d_rs.at[8 + i],
                    dev(x, (up, down)[way], mod8(z + i), core))

    def direct(i):
        return send(packed.at[rows_of(mod8(z + i), y_hi)], slot(z, y_hi),
                    d_ss.at[i], d_rs.at[i], dev(x, y, mod8(z + i), core))

    for i in (3, 4, 2, 5, 1, 6, 0, 7):
        go(first(i))
    for i in (4, 3, 5, 2, 6, 1, 7):
        go(direct(i))
    q_all[rows_of(z, y_hi), :] = packed[rows_of(z, y_hi), :]
    for i in (3, 4, 2, 5, 1, 6, 0, 7):
        first(i).wait_recv()
        go(second(i))
    for i in range(1, 8):
        direct(i).wait_recv()
    for i in range(8):
        second(i).wait_recv()

    row = lax.broadcasted_iota(jnp.int32, (256, 256), 0)
    col = lax.broadcasted_iota(jnp.int32, (256, 256), 1)
    same = lax.rem(col, 16) == row // 16
    swap = jnp.where(same & (col // 16 == lax.rem(row, 16)), HD ** -0.5, 0.0).astype(BF16)
    seen = same & (col // 16 <= lax.rem(row, 16))
    qp[...] = jnp.dot(swap, q_all[:, :WIDTH], preferred_element_type=F32).astype(BF16)
    for h in range(0, H, 2):
        pair = []
        for k in (h, h + 1):
            keys = q_all[:, WIDTH + k * HD:WIDTH + (k + 1) * HD]
            values = q_all[:, 2 * WIDTH + k * HD:2 * WIDTH + (k + 1) * HD]
            scores = lax.dot_general(qp[:, k * HD:(k + 1) * HD], keys, (((1,), (1,)), ((), ())),
                                     preferred_element_type=F32)
            scores = jnp.where(seen, scores, -1e30)
            expo = jnp.exp(scores - jnp.max(scores, axis=-1, keepdims=True))
            share = expo / jnp.sum(expo, axis=-1, keepdims=True)
            pair.append(jnp.dot(share.astype(BF16), values, preferred_element_type=F32))
        out[:, h * HD:(h + 2) * HD] = jnp.concatenate(pair, axis=1).astype(BF16)
    for copy in sent:
        copy.wait_send()


def depth_stage(tf, gain, w, emb, tok, dgain, qw):
    vmem = pl.BlockSpec(memory_space=pltpu.VMEM)
    dma = pltpu.SemaphoreType.DMA
    return pl.pallas_call(
        depth_kernel,
        name="depth",
        out_shape=jax.ShapeDtypeStruct((256, WIDTH), BF16),
        in_specs=[vmem] * 7,
        out_specs=vmem,
        scratch_shapes=[
            pltpu.VMEM((256, 512), BF16),
            pltpu.VMEM((256, 1024), F32),
            pltpu.VMEM((256, 3 * WIDTH), BF16),
            pltpu.VMEM((256, 3 * WIDTH), BF16),
            pltpu.VMEM((256, WIDTH), BF16),
            pltpu.VMEM((8, 16, 3 * WIDTH), BF16),
            dma((16,)), dma((16,)), dma((8,)), dma((8,)),
        ],
        compiler_params=pltpu.CompilerParams(collective_id=1, has_side_effects=True),
        cost_estimate=pl.CostEstimate(flops=4 * 10**9, bytes_accessed=20 * 2**20, transcendentals=0),
    )(tf, gain, w, emb, tok, dgain, qw)


def per_device(gate_pre, up_pre, down_weight, residual, out_gain, in_proj, embedding, token_ids,
               depth_gain, qkv_weight):
    own = jnp.concatenate(
        [in_proj[0], embedding[0], qkv_weight[0].reshape(48, 1024)], axis=0)
    every = lax.all_gather(own, "frames", axis=0)
    tf = mix(gate_pre, up_pre, down_weight, residual)
    w = every[:, :128].reshape(4096, 1024)
    emb = every[:, 128:160].reshape(1024, 1024)
    qw = every[:, 160:].reshape(1024, 1536)
    out = depth_stage(tf, out_gain.reshape(8, 1, 512), w, emb, token_ids, depth_gain, qw)
    return out.reshape(16, 16, WIDTH)


def solution(mesh):
    placed = (
        P("frames", "book"),
        P("frames", "book"),
        P("book", None),
        P("frames", "book"),
        P(),
        P("book", "frames", None),
        P("book", "frames", None),
        P("frames", "book"),
        P("book", None),
        P("book", "frames", None),
    )
    return jax.shard_map(per_device, mesh=mesh, in_specs=placed,
                         out_specs=P(("frames", "book"), None, None), check_vma=False)
```

```python
import jax
import jax.numpy as jnp
from jax import lax
from jax.experimental import pallas as pl
from jax.experimental.pallas import tpu as pltpu
from jax.sharding import PartitionSpec as P

H = 8
HD = 64
WIDTH = H * HD
MESH = pl.DeviceIdType.MESH
F32 = jnp.float32
BF16 = jnp.bfloat16
SHARD_ROWS = (128, 32, 32)


def dev(x, y, z, core):
    return {"frames": x * 8 + lax.rem(y, 4) * 2 + core, "book": z * 2 + y // 4}


def send(src, dst, ssem, rsem, target):
    return pltpu.make_async_remote_copy(
        src_ref=src, dst_ref=dst, send_sem=ssem, recv_sem=rsem,
        device_id=target, device_id_type=MESH,
    )


def mod8(v):
    return lax.rem(v + 16, 8)


def mod4(v):
    return lax.rem(v + 8, 4)


def kernel(gate_in, up_in, dw_in, res_in, gain, w_in, e_in, q_in, tok, dgain, out,
           gate, up, dw, res, hid, own, a_s, a_r, zs, ys, y_rel, y_r, tf, wbuf, ebuf, qbuf,
           xb, acc, looked, packed, q_all, qp, rel,
           in_sem, own_sem, a_ss, a_rs, y_ss, y_rs, b_ss, b_rs, c_ss, c_rs, p_rs,
           d_ss, d_rs, r_ss, r_rs):
    f = lax.axis_index("frames")
    b = lax.axis_index("book")
    core = lax.rem(f, 2)
    yl = lax.rem(f // 2, 4)
    x = f // 8
    y_hi = lax.rem(b, 2)
    z = b // 2
    y = y_hi * 4 + yl
    mid = (yl + 1) // 2 == 1
    order = (yl, yl + 1 - 2 * lax.rem(yl, 2), 2 - yl // 2, 3 * (1 - yl // 2))
    zn = (dev(x, y, mod8(z + 1), core), dev(x, y, mod8(z - 1), core))
    yn = (dev(x, mod8(y + 2), z, core), dev(x, mod8(y - 2), z, core))
    xn = (dev(mod4(x + 1), y, z, core), dev(mod4(x - 1), y, z, core))
    near = dev(x, y_hi * 4 + order[1], z, core)
    inner = dev(x, y_hi * 4 + 3 - yl, z, core)
    twin = dev(x, y, z, 1 - core)
    way_up, way_down = mod8(y + 2), mod8(y - 2)

    weights = (wbuf, ebuf, qbuf)
    shards = (w_in, e_in, q_in)

    def c_slot(a, bx, by, half=None, c=core):
        rows = SHARD_ROWS[a]
        start = ((bx * 4 + by) * 2 + c) * rows
        if half is not None:
            rows //= 2
            start = start + half * rows
        return weights[a].at[pl.ds(pl.multiple_of(start, rows), rows)]

    loads = [pltpu.make_async_copy(src, dst, in_sem.at[i]) for i, (src, dst) in enumerate(
        ((gate_in, gate), (up_in, up), (dw_in, dw), (res_in, res)))]
    places = [pltpu.make_async_copy(shards[a].at[0], c_slot(a, x, yl), own_sem.at[a])
              for a in range(3)]
    for copy in loads + places:
        copy.start()

    peers = [dev(x, y, mod8(z - i), core) for i in range(1, 8)]
    peers += [dev(x, way_down, mod8(z - i), core) for i in range(4)]
    peers += [dev(x, way_up, z, core)]
    peers += [dev(x, way_up, mod8(z - i), core) for i in range(4, 8)]
    peers += [xn[0], xn[1], near, twin]
    sem = pltpu.get_barrier_semaphore()
    for peer in peers:
        pl.semaphore_signal(sem, inc=1, device_id=peer, device_id_type=MESH)

    @pl.when(mid)
    def _():
        pl.semaphore_signal(sem, inc=1, device_id=inner, device_id_type=MESH)

    pl.semaphore_wait(sem, len(peers) + lax.rem((yl + 1) // 2, 2))

    sent = []
    sent_mid = []

    def go(copy):
        copy.start()
        sent.append(copy)

    def c_copy(a, n, src, bx, by, target, half=None):
        return send(src, c_slot(a, bx, by, half), c_ss.at[a, n],
                    c_rs.at[a, bx, by, 0 if half is None else half], target)

    def c_twin(a, n, src, bx, by):
        return send(src, c_slot(a, bx, by), c_ss.at[a, n], p_rs.at[a, bx, by], twin)

    def c_go_mid(copy):
        @pl.when(mid)
        def _():
            copy.start()
        sent_mid.append(copy)

    def c_own(a):
        src = shards[a].at[0]
        for d in (0, 1):
            go(c_copy(a, d, src, x, yl, xn[d]))
        go(c_copy(a, 2, src, x, yl, near))
        c_go_mid(c_copy(a, 3, src, x, yl, inner))
        go(c_twin(a, 4, src, x, yl))

    def c_wait(a, bx, by, half=None):
        c_copy(a, 0, c_slot(a, bx, by, half), bx, by, twin, half).wait_recv()

    def c_col(a, i):
        by = order[i]
        src = c_slot(a, x, by)
        c_wait(a, x, by)
        n = 5 + (i - 1) * 4
        for d in (0, 1):
            go(c_copy(a, n + d, src, x, by, xn[d]))
        target = dev(x, y_hi * 4 + (3 - yl), z, core) if i == 1 else dev(
            x, y_hi * 4 + mod4((yl - 1) * 3), z, core)
        c_go_mid(c_copy(a, n + 2, src, x, by, target))
        go(c_twin(a, n + 3, src, x, by))

    def c_row(a, i):
        by = order[i]
        n = 17 + i * 4
        for d in (0, 1):
            bx = mod4(x - 1) if d == 0 else mod4(x + 1)
            c_wait(a, bx, by)
            go(c_copy(a, n + d, c_slot(a, bx, by, d), bx, by, xn[d], d))
            go(c_twin(a, n + 2 + d, c_slot(a, bx, by), bx, by))

    def c_far(a, i):
        by = order[i]
        bx = mod4(x + 2)
        for half in (0, 1):
            c_wait(a, bx, by, half)
        go(c_twin(a, 33 + i, c_slot(a, bx, by), bx, by))

    def c_done(a):
        places[a].wait()
        for bx in range(4):
            for by in range(4):
                slot = c_slot(a, bx, by, None, 1 - core)
                send(slot, slot, c_ss.at[a, 0], p_rs.at[a, bx, by], twin).wait_recv()

    def a_copy(d, u, s):
        return send(a_s.at[d, u, s], a_r.at[d, u, s], a_ss.at[d, u, s], a_rs.at[d, u, s], zn[d])

    def y_copy(d, u):
        return send(ys.at[d, u], y_rel.at[d, u], y_ss.at[0, d, u], y_rs.at[0, d, u], yn[d])

    def y_copy2(d, u):
        return send(y_rel.at[d, u], y_r.at[d, u], y_ss.at[1, d, u], y_rs.at[1, d, u], yn[d])

    c_own(0)
    for copy in loads:
        copy.wait()
    g = gate[...].astype(F32)
    hid[...] = (g / (1.0 + jnp.exp(-g)) * up[...].astype(F32)).astype(BF16)

    def after_a(s):
        if s == 1:
            c_col(0, 1)
            c_row(0, 0)
        if s == 3:
            c_col(0, 2)
            c_row(0, 1)
            c_far(0, 0)
        if s == 5:
            c_col(0, 3)
            c_row(0, 2)
            c_far(0, 1)
            c_own(1)
            c_own(2)
        if s == 7:
            c_row(0, 3)
            c_far(0, 2)

    for s in range(8):
        for d in (0, 1):
            blk = mod8(z - 1 - s) if d == 0 else mod8(z + 1 + s)
            cols = pl.ds(pl.multiple_of(blk * 512, 512), 512)
            own[d] = jnp.dot(hid[d * 128:(d + 1) * 128, :], dw[:, cols],
                             preferred_element_type=F32).reshape(2, 64, 512)
        for u in (0, 1):
            for d in (0, 1):
                val = own[d, u]
                if s > 0:
                    a_copy(d, u, s - 1).wait_recv()
                    val = val + a_r[d, u, s - 1].astype(F32)
                if s < 7:
                    a_s[d, u, s] = val.astype(BF16)
                    go(a_copy(d, u, s))
                else:
                    zs[d, u] = val
                    cols = pl.ds(pl.multiple_of(y_hi * 256, 256), 256)
                    rows = pl.ds(d * 128 + u * 64, 64)
                    zs[d, u, :, cols] = zs[d, u, :, cols] + res[rows, :].astype(F32)
                    ys[d, u] = zs[d, u].astype(BF16)
                    go(y_copy(d, u))
        after_a(s)

    for u in (0, 1):
        for d in (0, 1):
            y_copy(d, u).wait_recv()
            go(y_copy2(d, u))
        if u == 0:
            c_far(0, 3)
            for a in (1, 2):
                c_col(a, 1)
                c_row(a, 0)

    def b_copy(d, s, h):
        blk = mod8(z - s) if d == 0 else mod8(z + s)
        ref = tf.at[blk, h]
        return send(ref, ref, b_ss.at[d, s, h], b_rs.at[d, s, h], zn[d])

    def block(i):
        v = tf[i].reshape(256, 512).astype(F32)
        cols = pl.ds(pl.multiple_of(i * 512, 512), 512)
        xb[...] = (v * gain[:, cols].astype(F32)).astype(BF16)

        def tile(n, carry):
            cols = pl.ds(pl.multiple_of(n * 256, 256), 256)
            rows = pl.ds(pl.multiple_of(i * 512, 512), 512)
            acc[:, cols] += jnp.dot(xb[...], wbuf[rows, cols], preferred_element_type=F32)
            return carry

        lax.fori_loop(0, 4, tile, 0)
        return jnp.sum(v * v, axis=-1, keepdims=True)

    for d in (0, 1):
        for u in (0, 1):
            y_copy2(d, u).wait_recv()
            tf[z, d, u * 64:(u + 1) * 64, :] = (zs[d, u] + y_r[d, u].astype(F32)).astype(BF16)
        for way in (0, 1):
            go(b_copy(way, 0, d))
    acc[...] = jnp.zeros_like(acc)
    for a in (1, 2):
        c_col(a, 2)
        c_row(a, 1)
        c_far(a, 0)
    total = jnp.zeros((256, 1), F32)
    for s in range(1, 5):
        for h in (0, 1):
            for d in (0, 1):
                if s == 4 and h != d:
                    continue
                b_copy(d, s - 1, h).wait_recv()
                if s < 3 or (s == 3 and h == d):
                    go(b_copy(d, s, h))
        if s == 1:
            for a in (1, 2):
                c_col(a, 3)
                c_row(a, 2)
                c_far(a, 1)
            c_done(0)
            total = total + block(z)
        if s == 2:
            for a in (1, 2):
                c_row(a, 3)
                c_far(a, 2)
        total = total + block(mod8(z - s))
        if s < 4:
            total = total + block(mod8(z + s))
        if s == 3:
            for a in (1, 2):
                c_far(a, 3)
            c_done(1)
            rows = lax.broadcasted_iota(jnp.int32, (1024, 256), 0)
            matches = jnp.where(tok[...] == rows, 1.0, 0.0).astype(BF16)
            looked[...] = lax.dot_general(matches, ebuf[...], (((0,), (0,)), ((), ())),
                                          preferred_element_type=F32)
            c_done(2)

    scale = lax.rsqrt(total * (1.0 / 4096) + 1e-05)
    depth = (acc[...] * scale + looked[...]).astype(BF16).astype(F32)
    moment = jnp.mean(depth * depth, axis=-1, keepdims=True)
    normed = (depth * lax.rsqrt(moment + 1e-05) * dgain[...].astype(F32)).astype(BF16)
    packed[...] = jnp.dot(normed, qbuf[...], preferred_element_type=F32).astype(BF16)

    def rows_of(zz, plane):
        return pl.ds(pl.multiple_of((zz * 2 + plane) * 16, 16), 16)

    def slot(zz, plane):
        return q_all.at[rows_of(zz, plane)]

    def first(i):
        return send(packed.at[rows_of(mod8(z + i), 1 - y_hi)], rel.at[i],
                    r_ss.at[i], r_rs.at[i], yn[i // 4])

    def second(i):
        source = (way_down, way_up)[i // 4] // 4
        return send(rel.at[i], slot(z, source), d_ss.at[8 + i], d_rs.at[8 + i],
                    dev(x, (way_up, way_down)[i // 4], mod8(z + i), core))

    def direct(i):
        return send(packed.at[rows_of(mod8(z + i), y_hi)], slot(z, y_hi),
                    d_ss.at[i], d_rs.at[i], dev(x, y, mod8(z + i), core))

    for i in (3, 4, 2, 5, 1, 6, 0, 7):
        go(first(i))
    for i in (4, 3, 5, 2, 6, 1, 7):
        go(direct(i))
    q_all[rows_of(z, y_hi), :] = packed[rows_of(z, y_hi), :]
    for i in (3, 4, 2, 5, 1, 6, 0, 7):
        first(i).wait_recv()
        go(second(i))
    for i in range(1, 8):
        direct(i).wait_recv()
    for i in range(8):
        second(i).wait_recv()

    row = lax.broadcasted_iota(jnp.int32, (256, 256), 0)
    col = lax.broadcasted_iota(jnp.int32, (256, 256), 1)
    same = lax.rem(col, 16) == row // 16
    swap = jnp.where(same & (col // 16 == lax.rem(row, 16)), HD ** -0.5, 0.0).astype(BF16)
    seen = same & (col // 16 <= lax.rem(row, 16))
    qp[...] = jnp.dot(swap, q_all[:, :WIDTH], preferred_element_type=F32).astype(BF16)
    for h in range(0, H, 2):
        pair = []
        for k in (h, h + 1):
            keys = q_all[:, WIDTH + k * HD:WIDTH + (k + 1) * HD]
            values = q_all[:, 2 * WIDTH + k * HD:2 * WIDTH + (k + 1) * HD]
            scores = lax.dot_general(qp[:, k * HD:(k + 1) * HD], keys, (((1,), (1,)), ((), ())),
                                     preferred_element_type=F32)
            scores = jnp.where(seen, scores, -1e30)
            expo = jnp.exp(scores - jnp.max(scores, axis=-1, keepdims=True))
            share = expo / jnp.sum(expo, axis=-1, keepdims=True)
            pair.append(jnp.dot(share.astype(BF16), values, preferred_element_type=F32))
        out[:, h * HD:(h + 2) * HD] = jnp.concatenate(pair, axis=1).astype(BF16)
    for copy in sent:
        copy.wait_send()

    @pl.when(mid)
    def _():
        for copy in sent_mid:
            copy.wait_send()


def per_device(gate_pre, up_pre, down_weight, residual, out_gain, in_proj, embedding, token_ids,
               depth_gain, qkv_weight):
    vmem = pl.BlockSpec(memory_space=pltpu.VMEM)
    whole = pl.BlockSpec(memory_space=pl.ANY)
    dma = pltpu.SemaphoreType.DMA
    out = pl.pallas_call(
        kernel,
        name="depth_step",
        out_shape=jax.ShapeDtypeStruct((256, WIDTH), BF16),
        in_specs=[whole] * 4 + [vmem] + [whole] * 3 + [vmem] * 2,
        out_specs=vmem,
        scratch_shapes=[
            pltpu.VMEM((256, 384), BF16),
            pltpu.VMEM((256, 384), BF16),
            pltpu.VMEM((384, 4096), BF16),
            pltpu.VMEM((256, 256), BF16),
            pltpu.VMEM((256, 384), BF16),
            pltpu.VMEM((2, 2, 64, 512), F32),
            pltpu.VMEM((2, 2, 7, 64, 512), BF16),
            pltpu.VMEM((2, 2, 7, 64, 512), BF16),
            pltpu.VMEM((2, 2, 64, 512), F32),
            pltpu.VMEM((2, 2, 64, 512), BF16),
            pltpu.VMEM((2, 2, 64, 512), BF16),
            pltpu.VMEM((2, 2, 64, 512), BF16),
            pltpu.VMEM((8, 2, 128, 512), BF16),
            pltpu.VMEM((4096, 1024), BF16),
            pltpu.VMEM((1024, 1024), BF16),
            pltpu.VMEM((1024, 3 * WIDTH), BF16),
            pltpu.VMEM((256, 512), BF16),
            pltpu.VMEM((256, 1024), F32),
            pltpu.VMEM((256, 1024), F32),
            pltpu.VMEM((256, 3 * WIDTH), BF16),
            pltpu.VMEM((256, 3 * WIDTH), BF16),
            pltpu.VMEM((256, WIDTH), BF16),
            pltpu.VMEM((8, 16, 3 * WIDTH), BF16),
            dma((4,)), dma((3,)),
            dma((2, 2, 7)), dma((2, 2, 7)),
            dma((2, 2, 2)), dma((2, 2, 2)),
            dma((2, 4, 2)), dma((2, 4, 2)),
            dma((3, 40)), dma((3, 4, 4, 2)), dma((3, 4, 4)),
            dma((16,)), dma((16,)), dma((8,)), dma((8,)),
        ],
        compiler_params=pltpu.CompilerParams(collective_id=0, has_side_effects=True),
    )(gate_pre, up_pre, down_weight, residual, out_gain.reshape(1, 4096), in_proj, embedding,
      qkv_weight, token_ids.reshape(1, 256), depth_gain)
    return out.reshape(16, 16, WIDTH)


def solution(mesh):
    placed = (
        P("frames", "book"),
        P("frames", "book"),
        P("book", None),
        P("frames", "book"),
        P(),
        P("book", "frames", None),
        P("book", "frames", None),
        P("frames", "book"),
        P("book", None),
        P("book", "frames", None),
    )
    return jax.shard_map(per_device, mesh=mesh, in_specs=placed,
                         out_specs=P(("frames", "book"), None, None), check_vma=False)
```

```python
import jax
import jax.numpy as jnp
from jax import lax
from jax.experimental import pallas as pl
from jax.experimental.pallas import tpu as pltpu
from jax.sharding import PartitionSpec as P

H = 8
HD = 64
WIDTH = H * HD
MESH = pl.DeviceIdType.MESH
F32 = jnp.float32
BF16 = jnp.bfloat16
SHARD_ROWS = (128, 32, 32)


def dev(x, y, z, core):
    return {"frames": x * 8 + lax.rem(y, 4) * 2 + core, "book": z * 2 + y // 4}


def send(src, dst, ssem, rsem, target):
    return pltpu.make_async_remote_copy(
        src_ref=src, dst_ref=dst, send_sem=ssem, recv_sem=rsem,
        device_id=target, device_id_type=MESH,
    )


def mod8(v):
    return lax.rem(v + 16, 8)


def mod4(v):
    return lax.rem(v + 8, 4)


def kernel(gate_in, up_in, dw_in, res_in, gain, w_in, e_in, q_in, tok, dgain, out,
           gate, up, dw, res, hid, own, a_s, a_r, zs, ys, y_rel, y_r, tf, wbuf, ebuf, qbuf,
           xs, acc, looked, packed, q_all, qp, rel,
           in_sem, own_sem, a_ss, a_rs, y_ss, y_rs, b_ss, b_rs, c_ss, c_rs, p_rs,
           d_ss, d_rs, r_ss, r_rs):
    f = lax.axis_index("frames")
    b = lax.axis_index("book")
    core = lax.rem(f, 2)
    yl = lax.rem(f // 2, 4)
    x = f // 8
    y_hi = lax.rem(b, 2)
    z = b // 2
    y = y_hi * 4 + yl
    mid = (yl + 1) // 2 == 1
    order = (yl, yl + 1 - 2 * lax.rem(yl, 2), 2 - yl // 2, 3 * (1 - yl // 2))
    zn = (dev(x, y, mod8(z + 1), core), dev(x, y, mod8(z - 1), core))
    yn = (dev(x, mod8(y + 2), z, core), dev(x, mod8(y - 2), z, core))
    xn = (dev(mod4(x + 1), y, z, core), dev(mod4(x - 1), y, z, core))
    near = dev(x, y_hi * 4 + order[1], z, core)
    inner = dev(x, y_hi * 4 + 3 - yl, z, core)
    twin = dev(x, y, z, 1 - core)
    way_up, way_down = mod8(y + 2), mod8(y - 2)

    weights = (wbuf, ebuf, qbuf)
    shards = (w_in, e_in, q_in)

    def c_slot(a, bx, by, half=None, c=core):
        rows = SHARD_ROWS[a]
        start = ((bx * 4 + by) * 2 + c) * rows
        if half is not None:
            rows //= 2
            start = start + half * rows
        return weights[a].at[pl.ds(pl.multiple_of(start, rows), rows)]

    loads = [pltpu.make_async_copy(src, dst, in_sem.at[i]) for i, (src, dst) in enumerate(
        ((gate_in, gate), (up_in, up), (dw_in, dw), (res_in, res)))]
    places = [pltpu.make_async_copy(shards[a].at[0], c_slot(a, x, yl), own_sem.at[a])
              for a in range(3)]
    for copy in loads + places:
        copy.start()

    peers = [dev(x, y, mod8(z - i), core) for i in range(1, 8)]
    peers += [dev(x, way_down, mod8(z - i), core) for i in range(4)]
    peers += [dev(x, way_up, z, core)]
    peers += [dev(x, way_up, mod8(z - i), core) for i in range(4, 8)]
    peers += [xn[0], xn[1], near, twin]
    sem = pltpu.get_barrier_semaphore()
    for peer in peers:
        pl.semaphore_signal(sem, inc=1, device_id=peer, device_id_type=MESH)

    @pl.when(mid)
    def _():
        pl.semaphore_signal(sem, inc=1, device_id=inner, device_id_type=MESH)

    for copy in loads:
        copy.wait()
    g = gate[...].astype(F32)
    hid[...] = (g / (1.0 + jnp.exp(-g)) * up[...].astype(F32)).astype(BF16)

    def product(s):
        for d in (0, 1):
            blk = mod8(z - 1 - s) if d == 0 else mod8(z + 1 + s)
            cols = pl.ds(pl.multiple_of(blk * 512, 512), 512)
            own[d] = jnp.dot(hid[d * 128:(d + 1) * 128, :], dw[:, cols],
                             preferred_element_type=F32).reshape(2, 64, 512)

    product(0)
    pl.semaphore_wait(sem, len(peers) + lax.rem((yl + 1) // 2, 2))

    sent = []
    sent_mid = []

    def go(copy):
        copy.start()
        sent.append(copy)

    def c_copy(a, n, src, bx, by, target, half=None):
        return send(src, c_slot(a, bx, by, half), c_ss.at[a, n],
                    c_rs.at[a, bx, by, 0 if half is None else half], target)

    def c_twin(a, n, src, bx, by):
        return send(src, c_slot(a, bx, by), c_ss.at[a, n], p_rs.at[a, bx, by], twin)

    def c_go_mid(copy):
        @pl.when(mid)
        def _():
            copy.start()
        sent_mid.append(copy)

    def c_own(a):
        src = shards[a].at[0]
        for d in (0, 1):
            go(c_copy(a, d, src, x, yl, xn[d]))
        go(c_copy(a, 2, src, x, yl, near))
        c_go_mid(c_copy(a, 3, src, x, yl, inner))
        go(c_twin(a, 4, src, x, yl))

    def c_wait(a, bx, by, half=None):
        c_copy(a, 0, c_slot(a, bx, by, half), bx, by, twin, half).wait_recv()

    def y_next(i):
        return inner if i == 1 else dev(x, y_hi * 4 + mod4((yl - 1) * 3), z, core)

    def c_col(a, i):
        by = order[i]
        src = c_slot(a, x, by)
        c_wait(a, x, by)
        n = 5 + (i - 1) * 4
        for d in (0, 1):
            go(c_copy(a, n + d, src, x, by, xn[d]))
        c_go_mid(c_copy(a, n + 2, src, x, by, y_next(i)))
        go(c_twin(a, n + 3, src, x, by))

    def c_row(a, i):
        by = order[i]
        n = 17 + i * 4
        for d in (0, 1):
            bx = mod4(x - 1) if d == 0 else mod4(x + 1)
            c_wait(a, bx, by)
            go(c_copy(a, n + d, c_slot(a, bx, by, d), bx, by, xn[d], d))
            go(c_twin(a, n + 2 + d, c_slot(a, bx, by), bx, by))

    def c_far(a, i):
        by = order[i]
        bx = mod4(x + 2)
        for half in (0, 1):
            c_wait(a, bx, by, half)
        go(c_twin(a, 33 + i, c_slot(a, bx, by), bx, by))

    def e_spread(n, bx):
        src = c_slot(1, bx, yl)
        go(c_copy(1, n, src, bx, yl, near))
        c_go_mid(c_copy(1, n + 1, src, bx, yl, inner))
        go(c_twin(1, n + 2, src, bx, yl))

    def e_row():
        for d in (0, 1):
            bx = mod4(x - 1) if d == 0 else mod4(x + 1)
            c_wait(1, bx, yl)
            go(c_copy(1, 5 + d, c_slot(1, bx, yl, d), bx, yl, xn[d], d))
            e_spread(7 + 3 * d, bx)

    def e_far():
        bx = mod4(x + 2)
        for half in (0, 1):
            c_wait(1, bx, yl, half)
        e_spread(13, bx)

    def e_col(i):
        by = order[i]
        for k, step in enumerate((0, 1, 3, 2)):
            bx = mod4(x + step)
            src = c_slot(1, bx, by)
            c_wait(1, bx, by)
            n = 16 + (i - 1) * 8 + 2 * k
            c_go_mid(c_copy(1, n, src, bx, by, y_next(i)))
            go(c_twin(1, n + 1, src, bx, by))

    def c_done(a, columns):
        for bx in columns:
            for by in range(4):
                slot = c_slot(a, bx, by, None, 1 - core)
                send(slot, slot, c_ss.at[a, 0], p_rs.at[a, bx, by], twin).wait_recv()

    def a_copy(d, u, s):
        return send(a_s.at[d, u, s], a_r.at[d, u, s], a_ss.at[d, u, s], a_rs.at[d, u, s], zn[d])

    def y_copy(d, u):
        return send(ys.at[d, u], y_rel.at[d, u], y_ss.at[0, d, u], y_rs.at[0, d, u], yn[d])

    def y_copy2(d, u):
        return send(y_rel.at[d, u], y_r.at[d, u], y_ss.at[1, d, u], y_rs.at[1, d, u], yn[d])

    for a in range(3):
        c_own(a)

    def after_a(s):
        if s == 2:
            c_row(0, 0)
            c_col(0, 1)
            e_row()
        if s == 3:
            c_row(2, 0)
            c_col(2, 1)
            e_far()
        if s == 5:
            c_col(0, 2)
            c_row(0, 1)
        if s == 6:
            c_col(2, 2)
            c_far(0, 0)
            c_far(2, 0)
        if s == 7:
            c_row(2, 1)
            e_col(1)

    for s in range(8):
        if s:
            product(s)
        for u in (0, 1):
            for d in (0, 1):
                val = own[d, u]
                if s > 0:
                    a_copy(d, u, s - 1).wait_recv()
                    val = val + a_r[d, u, s - 1].astype(F32)
                if s < 7:
                    a_s[d, u, s] = val.astype(BF16)
                    go(a_copy(d, u, s))
                else:
                    zs[d, u] = val
                    cols = pl.ds(pl.multiple_of(y_hi * 256, 256), 256)
                    rows = pl.ds(d * 128 + u * 64, 64)
                    zs[d, u, :, cols] = zs[d, u, :, cols] + res[rows, :].astype(F32)
                    ys[d, u] = zs[d, u].astype(BF16)
                    go(y_copy(d, u))
        after_a(s)

    for u in (0, 1):
        for d in (0, 1):
            y_copy(d, u).wait_recv()
            go(y_copy2(d, u))
    c_col(0, 3)
    c_col(2, 3)
    c_row(0, 2)

    def b_copy(d, s, h):
        blk = mod8(z - s) if d == 0 else mod8(z + s)
        ref = tf.at[blk, h]
        return send(ref, ref, b_ss.at[d, s, h], b_rs.at[d, s, h], zn[d])

    def scaled(i):
        v = tf[i].reshape(256, 512).astype(F32)
        cols = pl.ds(pl.multiple_of(i * 512, 512), 512)
        xs[:, cols] = (v * gain[:, cols].astype(F32)).astype(BF16)
        return jnp.sum(v * v, axis=-1, keepdims=True)

    def project(bx, first):
        depth = pl.ds(pl.multiple_of(bx * 1024, 1024), 1024)

        def tile(n, carry):
            cols = pl.ds(pl.multiple_of(n * 256, 256), 256)
            part = jnp.dot(xs[:, depth], wbuf[depth, cols], preferred_element_type=F32)
            acc[:, cols] = part if first else acc[:, cols] + part
            return carry

        lax.fori_loop(0, 4, tile, 0)

    def look_up(bx, first):
        depth = pl.ds(pl.multiple_of(bx * 256, 256), 256)
        rows = lax.broadcasted_iota(jnp.int32, (256, 256), 0) + bx * 256
        matches = jnp.where(tok[...] == rows, 1.0, 0.0).astype(BF16)
        part = lax.dot_general(matches, ebuf[depth], (((0,), (0,)), ((), ())),
                               preferred_element_type=F32)
        looked[...] = part if first else looked[...] + part

    for d in (0, 1):
        for u in (0, 1):
            y_copy2(d, u).wait_recv()
            tf[z, d, u * 64:(u + 1) * 64, :] = (zs[d, u] + y_r[d, u].astype(F32)).astype(BF16)
        for way in (0, 1):
            go(b_copy(way, 0, d))
    e_col(2)
    c_far(0, 1)
    c_far(2, 1)
    total = scaled(z)
    for s in range(1, 5):
        for h in (0, 1):
            for d in (0, 1):
                if s == 4 and h != d:
                    continue
                b_copy(d, s - 1, h).wait_recv()
                if s < 3 or (s == 3 and h == d):
                    go(b_copy(d, s, h))
        if s == 1:
            c_row(2, 2)
            e_col(3)
        if s == 2:
            c_row(0, 3)
        if s == 3:
            c_far(0, 2)
            c_far(2, 2)
        total = total + scaled(mod8(z - s))
        if s < 4:
            total = total + scaled(mod8(z + s))
    c_row(2, 3)
    for copy in places:
        copy.wait()
    ring = (x, mod4(x + 1), mod4(x + 3), mod4(x + 2))
    c_done(1, range(4))
    for i in range(4):
        if i == 3:
            c_far(0, 3)
            c_far(2, 3)
        c_done(0, ring[i:i + 1])
        project(ring[i], i == 0)
        look_up(ring[i], i == 0)
    c_done(2, range(4))

    scale = lax.rsqrt(total * (1.0 / 4096) + 1e-05)
    depth = (acc[...] * scale + looked[...]).astype(BF16).astype(F32)
    moment = jnp.mean(depth * depth, axis=-1, keepdims=True)
    normed = (depth * lax.rsqrt(moment + 1e-05) * dgain[...].astype(F32)).astype(BF16)
    packed[...] = jnp.dot(normed, qbuf[...], preferred_element_type=F32).astype(BF16)

    def rows_of(zz, plane):
        return pl.ds(pl.multiple_of((zz * 2 + plane) * 16, 16), 16)

    def slot(zz, plane):
        return q_all.at[rows_of(zz, plane)]

    def first(i):
        return send(packed.at[rows_of(mod8(z + i), 1 - y_hi)], rel.at[i],
                    r_ss.at[i], r_rs.at[i], yn[i // 4])

    def second(i):
        source = (way_down, way_up)[i // 4] // 4
        return send(rel.at[i], slot(z, source), d_ss.at[8 + i], d_rs.at[8 + i],
                    dev(x, (way_up, way_down)[i // 4], mod8(z + i), core))

    def direct(i):
        return send(packed.at[rows_of(mod8(z + i), y_hi)], slot(z, y_hi),
                    d_ss.at[i], d_rs.at[i], dev(x, y, mod8(z + i), core))

    for i in (3, 4, 2, 5, 1, 6, 0, 7):
        go(first(i))
    for i in (4, 3, 5, 2, 6, 1, 7):
        go(direct(i))
    q_all[rows_of(z, y_hi), :] = packed[rows_of(z, y_hi), :]
    for i in (3, 4, 2, 5, 1, 6, 0, 7):
        first(i).wait_recv()
        go(second(i))
    for i in range(1, 8):
        direct(i).wait_recv()
    for i in range(8):
        second(i).wait_recv()

    row = lax.broadcasted_iota(jnp.int32, (256, 256), 0)
    col = lax.broadcasted_iota(jnp.int32, (256, 256), 1)
    same = lax.rem(col, 16) == row // 16
    swap = jnp.where(same & (col // 16 == lax.rem(row, 16)), HD ** -0.5, 0.0).astype(BF16)
    seen = same & (col // 16 <= lax.rem(row, 16))
    qp[...] = jnp.dot(swap, q_all[:, :WIDTH], preferred_element_type=F32).astype(BF16)
    for h in range(0, H, 2):
        pair = []
        for k in (h, h + 1):
            keys = q_all[:, WIDTH + k * HD:WIDTH + (k + 1) * HD]
            values = q_all[:, 2 * WIDTH + k * HD:2 * WIDTH + (k + 1) * HD]
            scores = lax.dot_general(qp[:, k * HD:(k + 1) * HD], keys, (((1,), (1,)), ((), ())),
                                     preferred_element_type=F32)
            scores = jnp.where(seen, scores, -1e30)
            expo = jnp.exp(scores - jnp.max(scores, axis=-1, keepdims=True))
            share = expo / jnp.sum(expo, axis=-1, keepdims=True)
            pair.append(jnp.dot(share.astype(BF16), values, preferred_element_type=F32))
        out[:, h * HD:(h + 2) * HD] = jnp.concatenate(pair, axis=1).astype(BF16)
    for copy in sent:
        copy.wait_send()

    @pl.when(mid)
    def _():
        for copy in sent_mid:
            copy.wait_send()


def per_device(gate_pre, up_pre, down_weight, residual, out_gain, in_proj, embedding, token_ids,
               depth_gain, qkv_weight):
    vmem = pl.BlockSpec(memory_space=pltpu.VMEM)
    whole = pl.BlockSpec(memory_space=pl.ANY)
    dma = pltpu.SemaphoreType.DMA
    out = pl.pallas_call(
        kernel,
        name="depth_step",
        out_shape=jax.ShapeDtypeStruct((256, WIDTH), BF16),
        in_specs=[whole] * 4 + [vmem] + [whole] * 3 + [vmem] * 2,
        out_specs=vmem,
        scratch_shapes=[
            pltpu.VMEM((256, 384), BF16),
            pltpu.VMEM((256, 384), BF16),
            pltpu.VMEM((384, 4096), BF16),
            pltpu.VMEM((256, 256), BF16),
            pltpu.VMEM((256, 384), BF16),
            pltpu.VMEM((2, 2, 64, 512), F32),
            pltpu.VMEM((2, 2, 7, 64, 512), BF16),
            pltpu.VMEM((2, 2, 7, 64, 512), BF16),
            pltpu.VMEM((2, 2, 64, 512), F32),
            pltpu.VMEM((2, 2, 64, 512), BF16),
            pltpu.VMEM((2, 2, 64, 512), BF16),
            pltpu.VMEM((2, 2, 64, 512), BF16),
            pltpu.VMEM((8, 2, 128, 512), BF16),
            pltpu.VMEM((4096, 1024), BF16),
            pltpu.VMEM((1024, 1024), BF16),
            pltpu.VMEM((1024, 3 * WIDTH), BF16),
            pltpu.VMEM((256, 4096), BF16),
            pltpu.VMEM((256, 1024), F32),
            pltpu.VMEM((256, 1024), F32),
            pltpu.VMEM((256, 3 * WIDTH), BF16),
            pltpu.VMEM((256, 3 * WIDTH), BF16),
            pltpu.VMEM((256, WIDTH), BF16),
            pltpu.VMEM((8, 16, 3 * WIDTH), BF16),
            dma((4,)), dma((3,)),
            dma((2, 2, 7)), dma((2, 2, 7)),
            dma((2, 2, 2)), dma((2, 2, 2)),
            dma((2, 4, 2)), dma((2, 4, 2)),
            dma((3, 40)), dma((3, 4, 4, 2)), dma((3, 4, 4)),
            dma((16,)), dma((16,)), dma((8,)), dma((8,)),
        ],
        compiler_params=pltpu.CompilerParams(collective_id=0, has_side_effects=True),
    )(gate_pre, up_pre, down_weight, residual, out_gain.reshape(1, 4096), in_proj, embedding,
      qkv_weight, token_ids.reshape(1, 256), depth_gain)
    return out.reshape(16, 16, WIDTH)


def solution(mesh):
    placed = (
        P("frames", "book"),
        P("frames", "book"),
        P("book", None),
        P("frames", "book"),
        P(),
        P("book", "frames", None),
        P("book", "frames", None),
        P("frames", "book"),
        P("book", None),
        P("book", "frames", None),
    )
    return jax.shard_map(per_device, mesh=mesh, in_specs=placed,
                         out_specs=P(("frames", "book"), None, None), check_vma=False)
```

```python
import jax
import jax.numpy as jnp
from jax import lax
from jax.experimental import pallas as pl
from jax.experimental.pallas import tpu as pltpu
from jax.sharding import PartitionSpec as P

H = 8
HD = 64
WIDTH = H * HD
MESH = pl.DeviceIdType.MESH
F32 = jnp.float32
BF16 = jnp.bfloat16
SHARD_ROWS = (128, 32, 32)
PLAN = {
    "start": (("own", 0), ("own", 2), ("cy", 0),),
    "A0": (("cy", 1), ("cy", 2),),
    "A3": (("col", 1, 1), ("col", 0, 1), ("row", 0, 0), ("col", 0, 2),),
    "A4": (("col", 1, 2),),
    "A5": (("col", 2, 2), ("col", 2, 1),),
    "A6": (("row", 0, 1), ("col", 1, 3),),
    "A7": (("own", 1), ("col", 0, 3),),
    "Y0": (("row", 2, 0),),
    "Y1": (("row", 1, 1),),
    "B0": (("row", 1, 0),),
    "B1": (("row", 0, 2), ("far", 0, 0),),
    "B2": (("row", 1, 2), ("row", 0, 3),),
    "B2a": (("far", 1, 0), ("far", 1, 1), ("far", 2, 0),),
    "B3": (("col", 2, 3), ("row", 1, 3),),
    "C1": (("row", 2, 2), ("far", 0, 1),),
    "B4": (("far", 0, 2),),
    "C2": (("row", 2, 3), ("far", 0, 3), ("far", 1, 2), ("far", 2, 2),),
    "C3": (("far", 1, 3),),
    "P0": (("row", 2, 1), ("far", 2, 3),),
    "P3": (("far", 2, 1),),
}


def dev(x, y, z, core):
    return {"frames": x * 8 + lax.rem(y, 4) * 2 + core, "book": z * 2 + y // 4}


def send(src, dst, ssem, rsem, target):
    return pltpu.make_async_remote_copy(
        src_ref=src, dst_ref=dst, send_sem=ssem, recv_sem=rsem,
        device_id=target, device_id_type=MESH,
    )


def mod8(v):
    return lax.rem(v + 16, 8)


def mod4(v):
    return lax.rem(v + 8, 4)


def kernel(gate_in, up_in, dw_in, res_in, gain, w_in, e_in, q_in, tok, dgain, out,
           gate, up, dw, res, hid, own, a_s, a_r, zs, ys, y_rel, y_r, t_rel, tf, wbuf, ebuf, qbuf,
           gains, xs, acc, looked, packed, q_all, qp, rel,
           in_sem, own_sem, a_ss, a_rs, y_ss, y_rs, t_ss, t_rs, b_ss, b_rs, c_ss, c_rs, p_rs,
           d_ss, d_rs, r_ss, r_rs):
    f = lax.axis_index("frames")
    b = lax.axis_index("book")
    core = lax.rem(f, 2)
    yl = lax.rem(f // 2, 4)
    x = f // 8
    y_hi = lax.rem(b, 2)
    z = b // 2
    y = y_hi * 4 + yl
    mid = (yl + 1) // 2 == 1
    order = (yl, yl + 1 - 2 * lax.rem(yl, 2), 2 - yl // 2, 3 * (1 - yl // 2))
    zn = (dev(x, y, mod8(z + 1), core), dev(x, y, mod8(z - 1), core))
    yn = (dev(x, mod8(y + 2), z, core), dev(x, mod8(y - 2), z, core))
    xn = (dev(mod4(x + 1), y, z, core), dev(mod4(x - 1), y, z, core))
    near = dev(x, y_hi * 4 + order[1], z, core)
    inner = dev(x, y_hi * 4 + 3 - yl, z, core)
    twin = dev(x, y, z, 1 - core)
    way_up, way_down = mod8(y + 2), mod8(y - 2)

    weights = (wbuf, ebuf, qbuf)
    shards = (w_in, e_in, q_in)

    def c_slot(a, bx, by, half=None, c=core):
        rows = SHARD_ROWS[a]
        start = ((bx * 4 + by) * 2 + c) * rows
        if half is not None:
            rows //= 2
            start = start + half * rows
        return weights[a].at[pl.ds(pl.multiple_of(start, rows), rows)]

    loads = [pltpu.make_async_copy(src, dst, in_sem.at[i]) for i, (src, dst) in enumerate(
        ((gate_in, gate), (up_in, up), (dw_in, dw), (res_in, res)))]
    places = [pltpu.make_async_copy(shards[a].at[0], c_slot(a, x, yl), own_sem.at[a])
              for a in range(3)]
    for copy in loads + places:
        copy.start()

    peers = [dev(x, y, mod8(z - i), core) for i in range(1, 8)]
    peers += [dev(x, way_down, mod8(z - i), core) for i in range(4)]
    peers += [dev(x, way_up, z, core)]
    peers += [dev(x, way_up, mod8(z - i), core) for i in range(4, 8)]
    peers += [xn[0], xn[1], near, twin]
    sem = pltpu.get_barrier_semaphore()
    for peer in peers:
        pl.semaphore_signal(sem, inc=1, device_id=peer, device_id_type=MESH)

    @pl.when(mid)
    def _():
        pl.semaphore_signal(sem, inc=1, device_id=inner, device_id_type=MESH)

    for copy in loads:
        copy.wait()
    g = gate[...].astype(F32)
    hid[...] = (g / (1.0 + jnp.exp(-g)) * up[...].astype(F32)).astype(BF16)

    def product(s):
        for d in (0, 1):
            blk = mod8(z - 1 - s) if d == 0 else mod8(z + 1 + s)
            cols = pl.ds(pl.multiple_of(blk * 512, 512), 512)
            own[d] = jnp.dot(hid[d * 128:(d + 1) * 128, :], dw[:, cols],
                             preferred_element_type=F32).reshape(2, 64, 512)

    gains[...] = gain[...].astype(F32)
    product(0)
    pl.semaphore_wait(sem, len(peers) + lax.rem((yl + 1) // 2, 2))

    sent = []
    sent_mid = []

    def go(copy):
        copy.start()
        sent.append(copy)

    def c_copy(a, n, src, bx, by, target, half=None):
        return send(src, c_slot(a, bx, by, half), c_ss.at[a, n],
                    c_rs.at[a, bx, by, 0 if half is None else half], target)

    def c_twin(a, n, src, bx, by):
        return send(src, c_slot(a, bx, by), c_ss.at[a, n], p_rs.at[a, bx, by], twin)

    def c_own(a):
        src = shards[a].at[0]
        for d in (0, 1):
            go(c_copy(a, d, src, x, yl, xn[d]))
        go(c_twin(a, 4, src, x, yl))

    def c_go_mid(copy):
        @pl.when(mid)
        def _():
            copy.start()
        sent_mid.append(copy)

    def y_next(i):
        return inner if i == 1 else dev(x, y_hi * 4 + mod4((yl - 1) * 3), z, core)

    def c_along_y(a):
        src = shards[a].at[0]
        go(c_copy(a, 2, src, x, yl, near))
        c_go_mid(c_copy(a, 3, src, x, yl, inner))

    def c_wait(a, bx, by, half=None):
        c_copy(a, 0, c_slot(a, bx, by, half), bx, by, twin, half).wait_recv()

    def c_col(a, i):
        by = order[i]
        src = c_slot(a, x, by)
        c_wait(a, x, by)
        n = 5 + (i - 1) * 4
        for d in (0, 1):
            go(c_copy(a, n + d, src, x, by, xn[d]))
        c_go_mid(c_copy(a, n + 2, src, x, by, y_next(i)))
        go(c_twin(a, n + 3, src, x, by))

    def c_row(a, i):
        by = order[i]
        n = 17 + i * 4
        for d in (0, 1):
            bx = mod4(x - 1) if d == 0 else mod4(x + 1)
            c_wait(a, bx, by)
            go(c_copy(a, n + d, c_slot(a, bx, by, d), bx, by, xn[d], d))
            go(c_twin(a, n + 2 + d, c_slot(a, bx, by), bx, by))

    def c_far(a, i):
        by = order[i]
        bx = mod4(x + 2)
        for half in (0, 1):
            c_wait(a, bx, by, half)
        go(c_twin(a, 33 + i, c_slot(a, bx, by), bx, by))

    stages = {"own": c_own, "cy": c_along_y, "col": c_col, "row": c_row, "far": c_far}

    def pass_on(place):
        for stage, *which in PLAN.get(place, ()):
            stages[stage](*which)

    def c_done(a, columns):
        for bx in columns:
            for by in range(4):
                slot = c_slot(a, bx, by, None, 1 - core)
                send(slot, slot, c_ss.at[a, 0], p_rs.at[a, bx, by], twin).wait_recv()

    def a_copy(d, u, s):
        return send(a_s.at[d, u, s], a_r.at[d, u, s], a_ss.at[d, u, s], a_rs.at[d, u, s], zn[d])

    def y_copy(d, u):
        return send(ys.at[d, u], y_rel.at[d, u], y_ss.at[0, d, u], y_rs.at[0, d, u], yn[d])

    def y_copy2(d, u):
        return send(y_rel.at[d, u], y_r.at[d, u], y_ss.at[1, d, u], y_rs.at[1, d, u], yn[d])

    pass_on("start")
    for s in range(8):
        if s:
            product(s)
        for u in (0, 1):
            for d in (0, 1):
                val = own[d, u]
                if s > 0:
                    a_copy(d, u, s - 1).wait_recv()
                    val = val + a_r[d, u, s - 1].astype(F32)
                if s < 7:
                    a_s[d, u, s] = val.astype(BF16)
                    go(a_copy(d, u, s))
                else:
                    zs[d, u] = val
                    cols = pl.ds(pl.multiple_of((1 - y_hi) * 256, 256), 256)
                    ys[d, u] = zs[d, u, :, cols].astype(BF16)
                    go(y_copy(d, u))
        pass_on("A%d" % s)

    for u in (0, 1):
        for d in (0, 1):
            y_copy(d, u).wait_recv()
            go(y_copy2(d, u))
        pass_on("Y%d" % u)

    planes = (y_hi, 1 - y_hi)

    def b_copy(k, d, s, h):
        blk = (mod8(z - s) if d == 0 else mod8(z + s)) * 2 + planes[k]
        ref = tf.at[blk, h]
        return send(ref, ref, b_ss.at[k, d, s, h], b_rs.at[k, d, s, h], zn[d])

    def t_copy(d):
        return send(tf.at[b, d], t_rel.at[d], t_ss.at[0, d], t_rs.at[0, d], yn[d])

    def t_copy2(d):
        source = (way_down, way_up)[d] // 4
        return send(t_rel.at[d], tf.at[z * 2 + source, d], t_ss.at[1, d], t_rs.at[1, d], yn[d])

    def scaled(i):
        v = tf[i].reshape(256, 256).astype(F32)
        for j in (0, 1):
            cols = pl.ds(pl.multiple_of(i * 256 + j * 128, 128), 128)
            xs[:, cols] = (v[:, j * 128:(j + 1) * 128] * gains[pl.ds(i * 2 + j, 1), :]).astype(BF16)
        return jnp.sum(v * v, axis=-1, keepdims=True)

    def project(bx, first):
        depth = pl.ds(pl.multiple_of(bx * 1024, 1024), 1024)

        def tile(n, carry):
            cols = pl.ds(pl.multiple_of(n * 256, 256), 256)
            part = jnp.dot(xs[:, depth], wbuf[depth, cols], preferred_element_type=F32)
            acc[:, cols] = part if first else acc[:, cols] + part
            return carry

        lax.fori_loop(0, 4, tile, 0)

    def look_up(bx, first):
        depth = pl.ds(pl.multiple_of(bx * 256, 256), 256)
        rows = lax.broadcasted_iota(jnp.int32, (256, 256), 0) + bx * 256
        matches = jnp.where(tok[...] == rows, 1.0, 0.0).astype(BF16)
        part = lax.dot_general(matches, ebuf[depth], (((0,), (0,)), ((), ())),
                               preferred_element_type=F32)
        looked[...] = part if first else looked[...] + part

    def b_step(k, s):
        for h in (0, 1):
            for d in (0, 1):
                if s == 4 and h != d:
                    continue
                b_copy(k, d, s - 1, h).wait_recv()
                if s < 3 or (s == 3 and h == d):
                    go(b_copy(k, d, s, h))

    def scaled_pair(k, s):
        part = scaled(mod8(z - s) * 2 + planes[k])
        if 0 < s < 4:
            part = part + scaled(mod8(z + s) * 2 + planes[k])
        return part

    mine = pl.ds(pl.multiple_of(y_hi * 256, 256), 256)
    for d in (0, 1):
        for u in (0, 1):
            y_copy2(d, u).wait_recv()
            rows = pl.ds(d * 128 + u * 64, 64)
            whole = zs[d, u, :, mine] + y_r[d, u].astype(F32) + res[rows, :].astype(F32)
            tf[b, d, u * 64:(u + 1) * 64, :] = whole.astype(BF16)
        for way in (0, 1):
            go(b_copy(0, way, 0, d))
        go(t_copy(d))
    pass_on("B0")
    total = scaled_pair(0, 0)
    b_step(0, 1)
    pass_on("B1")
    for d in (0, 1):
        t_copy(d).wait_recv()
        go(t_copy2(d))
    pass_on("B1a")
    total = total + scaled_pair(0, 1)
    b_step(0, 2)
    pass_on("B2")
    total = total + scaled_pair(0, 2)
    for d in (0, 1):
        t_copy2(d).wait_recv()
        for way in (0, 1):
            go(b_copy(1, way, 0, d))
    pass_on("B2a")
    b_step(0, 3)
    pass_on("B3")
    total = total + scaled_pair(0, 3) + scaled_pair(1, 0)
    b_step(1, 1)
    pass_on("C1")
    total = total + scaled_pair(1, 1)
    b_step(0, 4)
    pass_on("B4")
    total = total + scaled_pair(0, 4)
    b_step(1, 2)
    pass_on("C2")
    total = total + scaled_pair(1, 2)
    b_step(1, 3)
    pass_on("C3")
    total = total + scaled_pair(1, 3)
    b_step(1, 4)
    total = total + scaled_pair(1, 4)
    for copy in places:
        copy.wait()
    ring = (x, mod4(x + 1), mod4(x + 3), mod4(x + 2))
    pass_on("P0")
    for i in range(4):
        if i == 3:
            pass_on("P3")
        for a in (0, 1):
            c_done(a, ring[i:i + 1])
        project(ring[i], i == 0)
        look_up(ring[i], i == 0)
    pass_on("Q")
    c_done(2, range(4))

    scale = lax.rsqrt(total * (1.0 / 4096) + 1e-05)
    depth = (acc[...] * scale + looked[...]).astype(BF16).astype(F32)
    moment = jnp.mean(depth * depth, axis=-1, keepdims=True)
    normed = (depth * lax.rsqrt(moment + 1e-05) * dgain[...].astype(F32)).astype(BF16)
    def rows_of(zz, plane):
        return pl.ds(pl.multiple_of((zz * 2 + plane) * 16, 16), 16)

    def slot(k, zz, plane):
        return q_all.at[k, rows_of(zz, plane)]

    def first(k, i):
        return send(packed.at[k, rows_of(mod8(z + i), 1 - y_hi)], rel.at[k, i],
                    r_ss.at[k, i], r_rs.at[k, i], yn[i // 4])

    def second(k, i):
        source = (way_down, way_up)[i // 4] // 4
        return send(rel.at[k, i], slot(k, z, source), d_ss.at[k, 8 + i], d_rs.at[k, 8 + i],
                    dev(x, (way_up, way_down)[i // 4], mod8(z + i), core))

    def direct(k, i):
        return send(packed.at[k, rows_of(mod8(z + i), y_hi)], slot(k, z, y_hi),
                    d_ss.at[k, i], d_rs.at[k, i], dev(x, y, mod8(z + i), core))

    for k in range(3):
        packed[k] = jnp.dot(normed, qbuf[:, k * WIDTH:(k + 1) * WIDTH],
                            preferred_element_type=F32).astype(BF16)
        for i in (3, 4, 2, 5, 1, 6, 0, 7):
            go(first(k, i))
        for i in (4, 3, 5, 2, 6, 1, 7):
            go(direct(k, i))
        q_all[k, rows_of(z, y_hi), :] = packed[k, rows_of(z, y_hi), :]
    for k in range(3):
        for i in (3, 4, 2, 5, 1, 6, 0, 7):
            first(k, i).wait_recv()
            go(second(k, i))
    for k in range(3):
        for i in range(1, 8):
            direct(k, i).wait_recv()
        for i in range(8):
            second(k, i).wait_recv()

    row = lax.broadcasted_iota(jnp.int32, (256, 256), 0)
    col = lax.broadcasted_iota(jnp.int32, (256, 256), 1)
    same = lax.rem(col, 16) == row // 16
    swap = jnp.where(same & (col // 16 == lax.rem(row, 16)), HD ** -0.5, 0.0).astype(BF16)
    seen = same & (col // 16 <= lax.rem(row, 16))
    qp[...] = jnp.dot(swap, q_all[0], preferred_element_type=F32).astype(BF16)
    for h in range(0, H, 2):
        pair = []
        for k in (h, h + 1):
            keys = q_all[1, :, k * HD:(k + 1) * HD]
            values = q_all[2, :, k * HD:(k + 1) * HD]
            scores = lax.dot_general(qp[:, k * HD:(k + 1) * HD], keys, (((1,), (1,)), ((), ())),
                                     preferred_element_type=F32)
            scores = jnp.where(seen, scores, -1e30)
            expo = jnp.exp(scores - jnp.max(scores, axis=-1, keepdims=True))
            share = expo / jnp.sum(expo, axis=-1, keepdims=True)
            pair.append(jnp.dot(share.astype(BF16), values, preferred_element_type=F32))
        out[:, h * HD:(h + 2) * HD] = jnp.concatenate(pair, axis=1).astype(BF16)
    for copy in sent:
        copy.wait_send()

    @pl.when(mid)
    def _():
        for copy in sent_mid:
            copy.wait_send()


def per_device(gate_pre, up_pre, down_weight, residual, out_gain, in_proj, embedding, token_ids,
               depth_gain, qkv_weight):
    vmem = pl.BlockSpec(memory_space=pltpu.VMEM)
    whole = pl.BlockSpec(memory_space=pl.ANY)
    dma = pltpu.SemaphoreType.DMA
    out = pl.pallas_call(
        kernel,
        name="depth_step",
        out_shape=jax.ShapeDtypeStruct((256, WIDTH), BF16),
        in_specs=[whole] * 4 + [vmem] + [whole] * 3 + [vmem] * 2,
        out_specs=vmem,
        scratch_shapes=[
            pltpu.VMEM((256, 384), BF16),
            pltpu.VMEM((256, 384), BF16),
            pltpu.VMEM((384, 4096), BF16),
            pltpu.VMEM((256, 256), BF16),
            pltpu.VMEM((256, 384), BF16),
            pltpu.VMEM((2, 2, 64, 512), F32),
            pltpu.VMEM((2, 2, 7, 64, 512), BF16),
            pltpu.VMEM((2, 2, 7, 64, 512), BF16),
            pltpu.VMEM((2, 2, 64, 512), F32),
            pltpu.VMEM((2, 2, 64, 256), BF16),
            pltpu.VMEM((2, 2, 64, 256), BF16),
            pltpu.VMEM((2, 2, 64, 256), BF16),
            pltpu.VMEM((2, 128, 256), BF16),
            pltpu.VMEM((16, 2, 128, 256), BF16),
            pltpu.VMEM((4096, 1024), BF16),
            pltpu.VMEM((1024, 1024), BF16),
            pltpu.VMEM((1024, 3 * WIDTH), BF16),
            pltpu.VMEM((32, 128), F32),
            pltpu.VMEM((256, 4096), BF16),
            pltpu.VMEM((256, 1024), F32),
            pltpu.VMEM((256, 1024), F32),
            pltpu.VMEM((3, 256, WIDTH), BF16),
            pltpu.VMEM((3, 256, WIDTH), BF16),
            pltpu.VMEM((256, WIDTH), BF16),
            pltpu.VMEM((3, 8, 16, WIDTH), BF16),
            dma((4,)), dma((3,)),
            dma((2, 2, 7)), dma((2, 2, 7)),
            dma((2, 2, 2)), dma((2, 2, 2)),
            dma((2, 2)), dma((2, 2)),
            dma((2, 2, 4, 2)), dma((2, 2, 4, 2)),
            dma((3, 40)), dma((3, 4, 4, 2)), dma((3, 4, 4)),
            dma((3, 16)), dma((3, 16)), dma((3, 8)), dma((3, 8)),
        ],
        compiler_params=pltpu.CompilerParams(collective_id=0, has_side_effects=True),
    )(gate_pre, up_pre, down_weight, residual, out_gain.reshape(32, 128), in_proj, embedding,
      qkv_weight, token_ids.reshape(1, 256), depth_gain)
    return out.reshape(16, 16, WIDTH)


def solution(mesh):
    placed = (
        P("frames", "book"),
        P("frames", "book"),
        P("book", None),
        P("frames", "book"),
        P(),
        P("book", "frames", None),
        P("book", "frames", None),
        P("frames", "book"),
        P("book", None),
        P("book", "frames", None),
    )
    return jax.shard_map(per_device, mesh=mesh, in_specs=placed,
                         out_specs=P(("frames", "book"), None, None), check_vma=False)
```
